32 devices in a mesh: groups: 2 (over y), frame: 4 (over z), quarter: 2 (over x), sub: 2 (over core).
Axes of the slice: x: 2, y: 2, z: 4, core: 2. Of those that a mesh axis runs over, the one named last changes fastest.
Arguments:
- queries: bfloat16 [16, 1024, 256], P(('groups', 'frame'), ('quarter', 'sub')), parts along dimension 0, may hold values from -36 to 36
- keys: bfloat16 [16, 1024, 256], P(('groups', 'frame'), ('quarter', 'sub')), parts along dimension 0, may hold values from -6 to 6
- values: bfloat16 [16, 1024, 256], P(('groups', 'frame'), ('quarter', 'sub')), parts along dimension 0, may hold values from -6 to 6
Outputs:
- attended: bfloat16 [16, 1024, 256], P(('groups', 'frame'), ('quarter', 'sub')), parts along dimension 0
The draws below stay inside these ranges and needn't reach their ends.
There are 2 independent parts, one for each index of `groups`. The reference program is written for one: setup_inputs(seed, part) draws one part's arguments, and reference() takes and returns one part's arrays. A program takes and returns all parts, laid end to end along the dimension named above; each array names one. Nothing has to cross between parts.
All inputs are finite; a program needn't handle non-finite values.
Results may differ from the reference program's by a relative error of at most 0.0028.
Values may be sent and summed in bfloat16 or wider, within the bound.
A program may use at most 64 MiB of HBM per device.

```python
import math
import jax
import jax.numpy as jnp
from jax import lax

HEAD_DIM = 128
STRIP = 16
FRAMES = 8
POS = 1024


def draw_keys(key, part):
    shape = (FRAMES, POS, 2 * HEAD_DIM)
    result = jnp.clip(jax.random.normal(jax.random.fold_in(key, 1), shape, jnp.float32), -6.0, 6.0)
    return result.astype(jnp.bfloat16)


def draw_queries(key, part):
    shape = (FRAMES, POS, 2 * HEAD_DIM)
    result = jnp.clip(3.0 * jax.random.normal(jax.random.fold_in(key, 201), shape, jnp.float32), -18.0, 18.0)
    return result.astype(jnp.bfloat16)


def block_scale(stream_key, shape, split, smallest, high):
    def one(axis_at, shards_of):
        steps = jax.random.uniform(jax.random.fold_in(jax.random.fold_in(stream_key, 6), axis_at), (shards_of,), jnp.float32, smallest / len(split), high / len(split))
        return jnp.repeat(jnp.exp(steps), shape[axis_at] // shards_of).reshape((-1,) + (1,) * (len(shape) - axis_at - 1))

    loudness = one(*split[0])
    for cut in split[1:]:
        loudness = loudness * one(*cut)
    return loudness


def normal_values(stream_key, extent, spread, reach, cuts=(), dtype=jnp.bfloat16):
    values = jax.random.normal(stream_key, extent, jnp.float32) * spread
    if len(cuts) > 0:
        values = block_scale(stream_key, extent, cuts, -0.22, 0.18) * values
    return jnp.clip(values, min=-reach, max=reach).astype(dtype)


def setup_inputs(seed: int = 0, part: int = 0) -> dict:
    seeds = jax.random.split(jax.random.key(seed), 4)
    part_keys = jax.random.split(jax.random.fold_in(seeds[3], part), 4)
    queries = draw_queries(jax.random.fold_in(jax.random.fold_in(seeds[3], part), 71), part)
    keys = draw_keys(jax.random.fold_in(jax.random.fold_in(seeds[3], part), 71), part)
    values = normal_values(part_keys[2], (FRAMES, POS, 2 * HEAD_DIM), 1.0, 6.0, ((0, 4), (1, 4)))
    return {"queries": queries, "keys": keys, "values": values}


def attend(query_rows, key_rows, value_rows):
    width = query_rows.shape[-1]
    scores = jnp.dot(query_rows, key_rows.T, preferred_element_type=jnp.float32) * (1.0 / math.sqrt(width))
    highest = lax.optimization_barrier(jnp.max(scores, axis=-1, keepdims=True))
    expo = jnp.exp(scores - highest)
    totals = lax.optimization_barrier(jnp.sum(expo, axis=-1, keepdims=True))
    mixed = jnp.dot(expo.astype(jnp.bfloat16), value_rows, preferred_element_type=jnp.float32)
    return (mixed / totals).astype(jnp.bfloat16)

def reference(queries, keys, values):
    block_rows = math.gcd(POS, 1024)
    block_count = POS // block_rows

    def spatial_frame(frame_data):
        query_frame, key_frame, value_frame = frame_data
        grouped = query_frame.reshape(block_count, block_rows, HEAD_DIM)
        mixed = lax.map(lambda block: attend(block, key_frame, value_frame), grouped)
        return mixed.reshape(POS, HEAD_DIM)
    spatial = lax.map(spatial_frame, (queries[..., :HEAD_DIM], keys[..., :HEAD_DIM], values[..., :HEAD_DIM]))
    strips_total = POS // STRIP

    def to_strips(array):
        part_two = array[..., HEAD_DIM:].reshape(FRAMES, strips_total, STRIP, HEAD_DIM)
        return part_two.transpose(1, 0, 2, 3).reshape(strips_total, FRAMES * STRIP, HEAD_DIM)

    def strip_attend(strip_data):
        return attend(strip_data[0], strip_data[1], strip_data[2])
    temporal = lax.map(strip_attend, (to_strips(queries), to_strips(keys), to_strips(values)))
    temporal = temporal.reshape(strips_total, FRAMES, STRIP, HEAD_DIM).transpose(1, 0, 2, 3).reshape(FRAMES, POS, HEAD_DIM)
    return jnp.concatenate([spatial, temporal], axis=-1)
```

```python
import functools
import math

import jax
import jax.numpy as jnp
from jax import lax
from jax.experimental import pallas as pl
from jax.experimental.pallas import tpu as pltpu
from jax.sharding import PartitionSpec as P

STRIP = 16
MESH = pl.DeviceIdType.MESH


def attend(query_rows, key_rows, value_rows, score_scale):
    scores = lax.dot_general(
        query_rows, key_rows, (((1,), (1,)), ((), ())), preferred_element_type=jnp.float32
    )
    highest = jnp.max(scores, axis=-1, keepdims=True)
    expo = jnp.exp((scores - highest) * score_scale)
    totals = jnp.sum(expo, axis=-1, keepdims=True)
    mixed = jnp.dot(expo.astype(jnp.bfloat16), value_rows, preferred_element_type=jnp.float32)
    return (mixed / totals).astype(jnp.bfloat16)


def attend_strips(keys, values, queries, score_scale):
    width = keys.shape[-1]
    strips = [slice(lower, lower + STRIP) for lower in range(0, keys.shape[1], STRIP)]
    scores = jnp.concatenate(
        [
            lax.dot_general(
                queries[:, strip].reshape(-1, width), keys[:, strip].reshape(-1, width),
                (((1,), (1,)), ((), ())), preferred_element_type=jnp.float32,
            )
            for strip in strips
        ]
    )
    highest = jnp.max(scores, axis=-1, keepdims=True)
    expo = jnp.exp((scores - highest) * score_scale)
    totals = jnp.sum(expo, axis=-1, keepdims=True)
    weights = expo.astype(jnp.bfloat16)
    count = queries.shape[0] * STRIP
    mixed = [
        jnp.dot(
            weights[place * count : (place + 1) * count], values[:, strip].reshape(-1, width),
            preferred_element_type=jnp.float32,
        )
        for place, strip in enumerate(strips)
    ]
    result = (jnp.concatenate(mixed) / totals).astype(jnp.bfloat16)
    return [result[place * count : (place + 1) * count] for place in range(len(strips))]


def wait_for(ref, sem):
    pltpu.make_async_copy(ref, ref, sem).wait()


def kernel(
    sizes,
    q_in, k_in, v_in, out,
    q_sp, kv_sp, tm, o_tm, o_sp,
    in_z, in_x, in_s,
    local_sem, z_send, z_recv, r_send, r_recv,
    x_send, x_recv, s_send, s_recv,
):
    n, nq, ns, frames, tokens, width, parts = sizes
    chunks = len(parts)
    starts = [sum(parts[:chunk]) for chunk in range(chunks)]
    rows = tokens // n
    score_scale = 1.0 / math.sqrt(width)
    me = lax.axis_index("frame")
    my_quarter = lax.axis_index("quarter")
    my_sub = lax.axis_index("sub")
    arrays = (q_in, k_in, v_in)
    first = slice(0, width)
    second = slice(width, 2 * width)
    my_frames = pl.ds(me * frames, frames)
    my_spatial = kv_sp.at[:, :, my_quarter, my_sub]
    axes = (("frame", me, n, in_z), ("quarter", my_quarter, nq, in_x), ("sub", my_sub, ns, in_s))

    barrier = pltpu.get_barrier_semaphore()
    for name, place, extent, _ in axes:
        for other in range(1, extent):
            @pl.when(other > place)
            def _(name=name, other=other):
                pl.semaphore_signal(barrier, inc=1, device_id={name: other}, device_id_type=MESH)

    below = me + my_quarter + my_sub

    @pl.when(below > 0)
    def _():
        pl.semaphore_wait(barrier, below)

    for name, place, extent, answers in axes:
        for other in range(extent - 1):
            @pl.when(other < place)
            def _(name=name, other=other, place=place, answers=answers):
                pl.semaphore_signal(
                    answers.at[place], inc=1, device_id={name: other}, device_id_type=MESH
                )

    def send_strips(owner):
        for chunk in range(chunks):
            for index in range(3):
                lower = owner * rows + starts[chunk]
                pltpu.make_async_remote_copy(
                    src_ref=arrays[index].at[:, lower : lower + parts[chunk], second],
                    dst_ref=tm.at[index, my_frames, pl.ds(starts[chunk], parts[chunk]), :],
                    send_sem=z_send.at[0],
                    recv_sem=z_recv.at[chunk],
                    device_id={"frame": owner},
                    device_id_type=MESH,
                ).start()

    for owner in range(n - 1):
        @pl.when(owner < me)
        def _(owner=owner):
            send_strips(owner)

    loads = [
        (q_in.at[:, :, first], q_sp, local_sem.at[0]),
        (k_in.at[:, :, first], kv_sp.at[0, :, my_quarter, my_sub], local_sem.at[1]),
        (v_in.at[:, :, first], kv_sp.at[1, :, my_quarter, my_sub], local_sem.at[1]),
    ]
    my_rows = pl.ds(pl.multiple_of(me * rows, STRIP), rows)
    for index in range(3):
        loads.append((arrays[index].at[:, my_rows, second], tm.at[index, my_frames], local_sem.at[2]))
    for load in loads:
        pltpu.make_async_copy(*load).start()

    for name, place, extent, answers in axes[1:]:
        for other in range(1, extent):
            @pl.when(other > place)
            def _(other=other, answers=answers):
                pl.semaphore_wait(answers.at[other], 1)

    def quarter_copy(index, frame, step):
        return pltpu.make_async_remote_copy(
            src_ref=arrays[index + 1].at[frame, :, first],
            dst_ref=kv_sp.at[index, frame, my_quarter, my_sub],
            send_sem=x_send.at[step - 1],
            recv_sem=x_recv.at[frame * (nq - 1) + step - 1],
            device_id={"quarter": lax.rem(my_quarter + step, nq)},
            device_id_type=MESH,
        )

    def sub_copy(index, frame, hop, quarter, source):
        return pltpu.make_async_remote_copy(
            src_ref=source,
            dst_ref=kv_sp.at[index, frame, quarter, my_sub],
            send_sem=s_send.at[hop - 1],
            recv_sem=s_recv.at[frame * (ns - 1) + hop - 1],
            device_id={"sub": lax.rem(my_sub + hop, ns)},
            device_id_type=MESH,
        )

    for frame in range(frames):
        for index in range(2):
            for step in range(1, nq):
                quarter_copy(index, frame, step).start()
            for hop in range(1, ns):
                source = arrays[index + 1].at[frame, :, first]
                sub_copy(index, frame, hop, my_quarter, source).start()

    for owner in range(1, n):
        @pl.when(owner > me)
        def _(owner=owner):
            pl.semaphore_wait(in_z.at[owner], 1)
            send_strips(owner)

    wait_for(q_sp, local_sem.at[0])
    wait_for(my_spatial, local_sem.at[1])
    wait_for(tm.at[:, my_frames], local_sem.at[2])

    def forward(frame):
        for step in range(1, nq):
            source = lax.rem(my_quarter + step, nq)
            landed = kv_sp.at[:, frame, source, my_sub]
            wait_for(landed, x_recv.at[frame * (nq - 1) + nq - step - 1])
            for index in range(2):
                for hop in range(1, ns):
                    sub_copy(index, frame, hop, source, kv_sp.at[index, frame, source, my_sub]).start()

    puts = []

    def put(source, target):
        puts.append(pltpu.make_async_copy(source, target, local_sem.at[3 + len(puts)]))
        puts[-1].start()

    def spatial_frame(frame):
        for step in range(1, ns):
            source = lax.rem(my_sub + step, ns)
            wait_for(kv_sp.at[:, frame, :, source], s_recv.at[frame * (ns - 1) + ns - step - 1])
        key_rows = kv_sp[0, frame].reshape(nq * ns * tokens, width)
        value_rows = kv_sp[1, frame].reshape(nq * ns * tokens, width)
        o_sp[frame] = attend(q_sp[frame], key_rows, value_rows, score_scale)
        put(o_sp.at[frame], out.at[frame, :, first])

    def temporal_chunk(chunk):
        here = slice(starts[chunk], starts[chunk] + parts[chunk])
        wait_for(tm.at[:, pl.ds(0, (n - 1) * frames), here], z_recv.at[chunk])
        block = tm[1, :, here, :], tm[2, :, here, :], tm[0, :, here, :]
        for place, mixed in enumerate(attend_strips(*block, score_scale)):
            strip = slice(starts[chunk] + place * STRIP, starts[chunk] + (place + 1) * STRIP)
            o_tm[:, strip, :] = mixed.reshape(n * frames, STRIP, width)
        lower = pl.multiple_of(me * rows + starts[chunk], STRIP)
        target = out.at[:, pl.ds(lower, parts[chunk]), second]
        for receiver in range(n):
            @pl.when(receiver != me)
            def _(receiver=receiver):
                pltpu.make_async_remote_copy(
                    src_ref=o_tm.at[pl.ds(receiver * frames, frames), here],
                    dst_ref=target,
                    send_sem=r_send.at[0],
                    recv_sem=r_recv.at[0],
                    device_id={"frame": receiver},
                    device_id_type=MESH,
                ).start()
        put(o_tm.at[my_frames, here], target)

    forward(0)
    spatial_frame(0)
    for frame in range(1, frames):
        forward(frame)
    for chunk in range(chunks):
        temporal_chunk(chunk)
    for frame in range(1, frames):
        spatial_frame(frame)

    others = pl.ds(0, (n - 1) * frames)
    wait_for(o_tm.at[others], r_recv.at[0])
    for copy in puts:
        copy.wait()
    wait_for(tm.at[:, others], z_send.at[0])
    wait_for(o_tm.at[others], r_send.at[0])
    for step in range(1, nq):
        wait_for(my_spatial, x_send.at[step - 1])
    for hop in range(1, ns):
        wait_for(kv_sp.at[:, :, :, my_sub], s_send.at[hop - 1])


def body(mesh, queries, keys, values):
    frames, tokens, both = queries.shape
    width = both // 2
    n, nq, ns = mesh.shape["frame"], mesh.shape["quarter"], mesh.shape["sub"]
    rows = tokens // n
    parts = (rows,)
    chunks = len(parts)
    bf16 = jnp.bfloat16
    dma = pltpu.SemaphoreType.DMA
    regular = pltpu.SemaphoreType.REGULAR
    own = pltpu.VMEM((frames, tokens, width), bf16)
    return pl.pallas_call(
        functools.partial(kernel, (n, nq, ns, frames, tokens, width, parts)),
        out_shape=jax.ShapeDtypeStruct(queries.shape, bf16),
        in_specs=[pl.BlockSpec(memory_space=pltpu.HBM)] * 3,
        out_specs=pl.BlockSpec(memory_space=pl.ANY),
        scratch_shapes=[
            own,
            pltpu.VMEM((2, frames, nq, ns, tokens, width), bf16),
            pltpu.VMEM((3, n * frames, rows, width), bf16),
            pltpu.VMEM((n * frames, rows, width), bf16),
            own,
            regular((n,)), regular((nq,)), regular((ns,)),
            dma((3 + frames + chunks,)),
            dma((1,)), dma((chunks,)), dma((1,)), dma((1,)),
            dma((nq - 1,)), dma((frames * (nq - 1),)),
            dma((ns - 1,)), dma((frames * (ns - 1),)),
        ],
        compiler_params=pltpu.CompilerParams(collective_id=0, has_side_effects=True, vmem_limit_bytes=24 << 20),
    )(*[pltpu.with_memory_space_constraint(a, pltpu.HBM) for a in (queries, keys, values)])


def solution(mesh):
    spec = P(("groups", "frame"), ("quarter", "sub"), None)
    return jax.shard_map(
        functools.partial(body, mesh),
        mesh=mesh,
        in_specs=(spec, spec, spec),
        out_specs=spec,
        check_vma=False,
    )
```

```python
import functools
import math

import jax
import jax.numpy as jnp
from jax import lax
from jax.experimental import pallas as pl
from jax.experimental.pallas import tpu as pltpu
from jax.sharding import PartitionSpec as P

STRIP = 16
MESH = pl.DeviceIdType.MESH


def attend(query_rows, key_rows, value_rows, score_scale):
    scores = lax.dot_general(
        query_rows, key_rows, (((1,), (1,)), ((), ())), preferred_element_type=jnp.float32
    )
    highest = jnp.max(scores, axis=-1, keepdims=True)
    expo = jnp.exp((scores - highest) * score_scale)
    totals = jnp.sum(expo, axis=-1, keepdims=True)
    mixed = jnp.dot(expo.astype(jnp.bfloat16), value_rows, preferred_element_type=jnp.float32)
    return (mixed / totals).astype(jnp.bfloat16)


def attend_strips(keys, values, queries, score_scale):
    width = keys.shape[-1]
    strips = [slice(lower, lower + STRIP) for lower in range(0, keys.shape[1], STRIP)]
    scores = jnp.concatenate(
        [
            lax.dot_general(
                queries[:, strip].reshape(-1, width), keys[:, strip].reshape(-1, width),
                (((1,), (1,)), ((), ())), preferred_element_type=jnp.float32,
            )
            for strip in strips
        ]
    )
    highest = jnp.max(scores, axis=-1, keepdims=True)
    expo = jnp.exp((scores - highest) * score_scale)
    totals = jnp.sum(expo, axis=-1, keepdims=True)
    weights = expo.astype(jnp.bfloat16)
    count = queries.shape[0] * STRIP
    mixed = [
        jnp.dot(
            weights[place * count : (place + 1) * count], values[:, strip].reshape(-1, width),
            preferred_element_type=jnp.float32,
        )
        for place, strip in enumerate(strips)
    ]
    result = (jnp.concatenate(mixed) / totals).astype(jnp.bfloat16)
    return [result[place * count : (place + 1) * count] for place in range(len(strips))]


def wait_for(ref, sem):
    pltpu.make_async_copy(ref, ref, sem).wait()


def kernel(
    sizes,
    q_in, k_in, v_in, out,
    q_sp, kv_sp, tm, o_tm, o_sp,
    in_z, in_x, in_s,
    local_sem, cross_send, cross_recv, own_send, own_recv, r_send, r_recv,
    x_send, x_recv, s_send, s_recv,
):
    n, nq, ns, frames, tokens, width, parts = sizes
    chunks = len(parts)
    starts = [sum(parts[:chunk]) for chunk in range(chunks)]
    half = n // 2
    rows = tokens // half
    score_scale = 1.0 / math.sqrt(width)
    me = lax.axis_index("frame")
    my_quarter = lax.axis_index("quarter")
    my_sub = lax.axis_index("sub")
    upper = (me >= half).astype(jnp.int32)
    base = upper * half
    mine = me - base
    arrays = (q_in, k_in, v_in)
    first = slice(0, width)
    second = slice(width, 2 * width)
    my_frames = pl.ds(me * frames, frames)
    my_spatial = kv_sp.at[:, :, my_quarter, my_sub]
    axes = (("frame", me, n, in_z), ("quarter", my_quarter, nq, in_x), ("sub", my_sub, ns, in_s))

    barrier = pltpu.get_barrier_semaphore()
    for name, place, extent, _ in axes:
        for other in range(1, extent):
            @pl.when(other > place)
            def _(name=name, other=other):
                pl.semaphore_signal(barrier, inc=1, device_id={name: other}, device_id_type=MESH)

    below = me + my_quarter + my_sub

    @pl.when(below > 0)
    def _():
        pl.semaphore_wait(barrier, below)

    for name, place, extent, answers in axes:
        for other in range(extent - 1):
            @pl.when(other < place)
            def _(name=name, other=other, place=place, answers=answers):
                pl.semaphore_signal(
                    answers.at[place], inc=1, device_id={name: other}, device_id_type=MESH
                )

    def strip_copy(index, chunk, owner, send_sem, recv_sem):
        lower = lax.rem(owner, half) * rows + starts[chunk]
        return pltpu.make_async_remote_copy(
            src_ref=arrays[index].at[:, pl.ds(pl.multiple_of(lower, STRIP), parts[chunk]), second],
            dst_ref=tm.at[index, my_frames, pl.ds(starts[chunk], parts[chunk]), :],
            send_sem=send_sem,
            recv_sem=recv_sem,
            device_id={"frame": owner},
            device_id_type=MESH,
        )

    down = [(owner, chunk) for owner in range(half - 1, -1, -1) for chunk in range(chunks)]
    up = [(owner, chunk) for owner in range(n - 1, half - 1, -1) for chunk in range(chunks)]
    up.insert(0, up.pop(up.index((half, 0))))

    def send_cross(entries, known):
        for owner, chunk in entries:
            if owner not in known:
                pl.semaphore_wait(in_z.at[owner], 1)
                known.add(owner)
            for index in (1, 2):
                strip_copy(index, chunk, owner, cross_send.at[0], cross_recv.at[chunk]).start()

    soon, later = down[: len(down) // 2], down[len(down) // 2 :]
    below_half = set(range(half))

    @pl.when(upper == 1)
    def _():
        send_cross(soon, below_half)

    @pl.when((upper == 1) & (my_sub == 0))
    def _():
        send_cross(later, below_half)

    def neighbour(step):
        return base + lax.rem(mine + step, half)

    for step in range(1, half):
        @pl.when(neighbour(step) > me)
        def _(step=step):
            pl.semaphore_wait(in_z.at[neighbour(step)], 1)

        for chunk in range(chunks):
            for index in range(3):
                strip_copy(
                    index, chunk, neighbour(step),
                    own_send.at[step - 1], own_recv.at[chunk * (half - 1) + step - 1],
                ).start()

    loads = [
        (q_in.at[:, :, first], q_sp, local_sem.at[0]),
        (k_in.at[:, :, first], kv_sp.at[0, :, my_quarter, my_sub], local_sem.at[1]),
        (v_in.at[:, :, first], kv_sp.at[1, :, my_quarter, my_sub], local_sem.at[1]),
    ]
    my_rows = pl.ds(pl.multiple_of(mine * rows, STRIP), rows)
    for index in range(3):
        loads.append((arrays[index].at[:, my_rows, second], tm.at[index, my_frames], local_sem.at[2]))
    for load in loads:
        pltpu.make_async_copy(*load).start()

    for name, place, extent, answers in axes[1:]:
        for other in range(1, extent):
            @pl.when(other > place)
            def _(other=other, answers=answers):
                pl.semaphore_wait(answers.at[other], 1)

    def quarter_copy(index, frame, step):
        return pltpu.make_async_remote_copy(
            src_ref=arrays[index + 1].at[frame, :, first],
            dst_ref=kv_sp.at[index, frame, my_quarter, my_sub],
            send_sem=x_send.at[step - 1],
            recv_sem=x_recv.at[frame * (nq - 1) + step - 1],
            device_id={"quarter": lax.rem(my_quarter + step, nq)},
            device_id_type=MESH,
        )

    def sub_copy(index, frame, hop, quarter, source):
        return pltpu.make_async_remote_copy(
            src_ref=source,
            dst_ref=kv_sp.at[index, frame, quarter, my_sub],
            send_sem=s_send.at[hop - 1],
            recv_sem=s_recv.at[frame * (ns - 1) + hop - 1],
            device_id={"sub": lax.rem(my_sub + hop, ns)},
            device_id_type=MESH,
        )

    for frame in range(frames):
        for index in range(2):
            for step in range(1, nq):
                quarter_copy(index, frame, step).start()
            for hop in range(1, ns):
                source = arrays[index + 1].at[frame, :, first]
                sub_copy(index, frame, hop, my_quarter, source).start()

    @pl.when((upper == 1) & (my_sub > 0))
    def _():
        send_cross(later, below_half)

    @pl.when(upper == 0)
    def _():
        send_cross(up, set())

    wait_for(q_sp, local_sem.at[0])
    wait_for(my_spatial, local_sem.at[1])
    wait_for(tm.at[:, my_frames], local_sem.at[2])

    def forward(frame):
        for step in range(1, nq):
            source = lax.rem(my_quarter + step, nq)
            landed = kv_sp.at[:, frame, source, my_sub]
            wait_for(landed, x_recv.at[frame * (nq - 1) + nq - step - 1])
            for index in range(2):
                for hop in range(1, ns):
                    sub_copy(index, frame, hop, source, kv_sp.at[index, frame, source, my_sub]).start()

    puts = []

    def put(source, target):
        puts.append(pltpu.make_async_copy(source, target, local_sem.at[3 + len(puts)]))
        puts[-1].start()

    def spatial_frame(frame):
        for step in range(1, ns):
            source = lax.rem(my_sub + step, ns)
            wait_for(kv_sp.at[:, frame, :, source], s_recv.at[frame * (ns - 1) + ns - step - 1])
        key_rows = kv_sp[0, frame].reshape(nq * ns * tokens, width)
        value_rows = kv_sp[1, frame].reshape(nq * ns * tokens, width)
        o_sp[frame] = attend(q_sp[frame], key_rows, value_rows, score_scale)
        put(o_sp.at[frame], out.at[frame, :, first])

    def temporal_chunk(chunk):
        here = slice(starts[chunk], starts[chunk] + parts[chunk])
        for step in range(1, half):
            sender = pl.ds(neighbour(step) * frames, frames)
            wait_for(tm.at[:, sender, here], own_recv.at[chunk * (half - 1) + half - step - 1])
        wait_for(
            tm.at[1:3, pl.ds((half - base) * frames, half * frames), here], cross_recv.at[chunk]
        )
        asked = pl.ds(base * frames, half * frames)
        block = tm[1, :, here, :], tm[2, :, here, :], tm[0, asked, here, :]
        for place, mixed in enumerate(attend_strips(*block, score_scale)):
            strip = slice(starts[chunk] + place * STRIP, starts[chunk] + (place + 1) * STRIP)
            o_tm[:, strip, :] = mixed.reshape(half * frames, STRIP, width)
        lower = pl.multiple_of(mine * rows + starts[chunk], STRIP)
        target = out.at[:, pl.ds(lower, parts[chunk]), second]
        for step in range(1, half):
            receiver = lax.rem(mine + step, half)
            pltpu.make_async_remote_copy(
                src_ref=o_tm.at[pl.ds(receiver * frames, frames), here],
                dst_ref=target,
                send_sem=r_send.at[step - 1],
                recv_sem=r_recv.at[step - 1],
                device_id={"frame": neighbour(step)},
                device_id_type=MESH,
            ).start()
        put(o_tm.at[pl.ds(mine * frames, frames), here], target)

    forward(0)
    spatial_frame(0)
    for frame in range(1, frames):
        forward(frame)
    temporal_chunk(0)
    for frame in range(1, frames):
        spatial_frame(frame)
    for chunk in range(1, chunks):
        temporal_chunk(chunk)

    for step in range(1, half):
        lower = pl.multiple_of(lax.rem(mine + step, half) * rows, STRIP)
        wait_for(out.at[:, pl.ds(lower, rows), second], r_recv.at[half - step - 1])
    for copy in puts:
        copy.wait()
    wait_for(my_spatial, cross_send.at[0])
    for step in range(1, half):
        wait_for(tm.at[:, my_frames], own_send.at[step - 1])
        wait_for(o_tm.at[pl.ds(0, frames)], r_send.at[step - 1])
    for step in range(1, nq):
        wait_for(my_spatial, x_send.at[step - 1])
    for hop in range(1, ns):
        wait_for(kv_sp.at[:, :, :, my_sub], s_send.at[hop - 1])


def split_rows(rows):
    pieces = math.gcd(rows // STRIP, 4)
    return (rows // pieces,) * pieces


def body(mesh, queries, keys, values):
    frames, tokens, both = queries.shape
    width = both // 2
    n, nq, ns = mesh.shape["frame"], mesh.shape["quarter"], mesh.shape["sub"]
    half = n // 2
    rows = tokens // half
    parts = split_rows(rows)
    chunks = len(parts)
    bf16 = jnp.bfloat16
    dma = pltpu.SemaphoreType.DMA
    regular = pltpu.SemaphoreType.REGULAR
    own = pltpu.VMEM((frames, tokens, width), bf16)
    return pl.pallas_call(
        functools.partial(kernel, (n, nq, ns, frames, tokens, width, parts)),
        out_shape=jax.ShapeDtypeStruct(queries.shape, bf16),
        in_specs=[pl.BlockSpec(memory_space=pltpu.HBM)] * 3,
        out_specs=pl.BlockSpec(memory_space=pl.ANY),
        scratch_shapes=[
            own,
            pltpu.VMEM((2, frames, nq, ns, tokens, width), bf16),
            pltpu.VMEM((3, n * frames, rows, width), bf16),
            pltpu.VMEM((half * frames, rows, width), bf16),
            own,
            regular((n,)), regular((nq,)), regular((ns,)),
            dma((3 + frames + chunks,)),
            dma((1,)), dma((chunks,)),
            dma((half - 1,)), dma((chunks * (half - 1),)),
            dma((half - 1,)), dma((half - 1,)),
            dma((nq - 1,)), dma((frames * (nq - 1),)),
            dma((ns - 1,)), dma((frames * (ns - 1),)),
        ],
        compiler_params=pltpu.CompilerParams(collective_id=0, has_side_effects=True, vmem_limit_bytes=24 << 20),
    )(*[pltpu.with_memory_space_constraint(a, pltpu.HBM) for a in (queries, keys, values)])


def solution(mesh):
    spec = P(("groups", "frame"), ("quarter", "sub"), None)
    return jax.shard_map(
        functools.partial(body, mesh),
        mesh=mesh,
        in_specs=(spec, spec, spec),
        out_specs=spec,
        check_vma=False,
    )
```
